32 devices in a mesh: groups: 2 (over y), tiles: 4 (over z), folds: 2 (over x), sub: 2 (over core).
Axes of the slice: x: 2, y: 2, z: 4, core: 2. Of those that a mesh axis runs over, the one named last changes fastest.
Arguments:
- features: bfloat16 [2, 32, 16, 16, 1024], P('folds', ('groups', 'tiles', 'sub')), parts along dimension 1, may hold values from -6 to 6
- conv_first: bfloat16 [2, 3, 3, 3, 64, 32], P('folds'), may hold values from -0.15625 to 0.15625
- gain_first: float32 [2, 32], P('folds'), may hold values from 0.1 to 1.9
- shift_first: float32 [2, 32], P('folds'), may hold values from -3 to 3
- conv_second: bfloat16 [2, 3, 3, 3, 32, 32], P('folds'), may hold values from -0.21875 to 0.21875
- gain_second: float32 [2, 32], P('folds'), may hold values from 0.1 to 1.9
- shift_second: float32 [2, 32], P('folds'), may hold values from -3 to 3
- head_weight: bfloat16 [2, 32, 16], P('folds'), may hold values from -1 to 1
- head_bias: float32 [2, 16], P('folds'), may hold values from -4 to 4
- corners: int32 [32, 3], P(('groups', 'tiles', 'sub')), parts along dimension 0, may hold values from 0 to 48, as said below
- counts: int32 [8, 2], P('groups'), parts along dimension 0, may hold values from 0 to 2, as said below
Outputs:
- logits: float32 [128, 40, 640], P(('groups', 'tiles'), ('folds', 'sub')), parts along dimension 0
The draws below stay inside these ranges and needn't reach their ends.
There are 2 independent parts, one for each index of `groups`. The reference program is written for one: setup_inputs(seed, part) draws one part's arguments, and reference() takes and returns one part's arrays. A program takes and returns all parts, laid end to end along the dimension named above; an argument that names none is the same for every part. Nothing has to cross between parts.
Inputs may be any that keep to these rules, and one draw needn't show every extreme that they name: `corners`: for slot n = (t * 2 + s) * 2 + j, the z coordinate lies in [t * 16, (t + 1) * 16) and equals (3) * 16 in the last slab; x lies in [0, 24] and y in [0, 24]. counts[t, s] + counts[t xor (2), s] <= 2 for every t and s; some entry equals 2.
All inputs are finite; a program needn't handle non-finite values.
Results may differ from the reference program's by a relative error of at most 0.01.
Values may be sent and summed in bfloat16 or wider, within the bound.
A program may use at most 128 MiB of HBM per device.

```python
import jax
import jax.numpy as jnp
from jax import lax

CIN = 64
CH = 32
CLASSES = 16
WE = 16
CAP = 2
TZ = 16
VX = 40
VY = 40
FOLDS = 2
TILES = 4
HALVES = 2
WINDOWS = 16
VZ = 64


def draw_counts(key, part):
    subkeys = jax.random.split(jax.random.fold_in(key, 17), 5)
    half_tiles = TILES // 2
    grid_shape = (half_tiles, HALVES)
    totals = jax.random.randint(subkeys[0], grid_shape, CAP // 2, CAP + 1)
    lower_part = jax.random.randint(subkeys[1], grid_shape, 0, totals + 1)
    chosen_tile = jax.random.randint(subkeys[2], (), 0, half_tiles)
    chosen_half = jax.random.randint(subkeys[3], (), 0, HALVES)
    upper_side = jax.random.randint(subkeys[4], (), 0, 2)
    marked = (jnp.arange(half_tiles)[:, None] == chosen_tile) & (jnp.arange(HALVES)[None, :] == chosen_half)
    totals = jnp.where(marked, CAP, totals)
    lower_part = jnp.where(marked, CAP * (1 - upper_side), lower_part)
    return jnp.concatenate([lower_part, totals - lower_part], axis=0).astype(jnp.int32)


def draw_corners(key, part):
    subkeys = jax.random.split(jax.random.fold_in(key, 29), 3)
    total_windows = TILES * HALVES * CAP
    owner_tile = jnp.arange(total_windows) // (HALVES * CAP)
    offsets = jax.random.randint(subkeys[0], (total_windows,), 0, TZ)
    offsets = jnp.where(owner_tile == TILES - 1, 0, offsets)
    depth = owner_tile * TZ + offsets
    across = jax.random.randint(subkeys[1], (total_windows,), 0, VX - WE + 1)
    along = jax.random.randint(subkeys[2], (total_windows,), 0, VY - WE + 1)
    return jnp.stack([depth, across, along], axis=1).astype(jnp.int32)


def block_scale(rng, extent, shards, smallest, largest):
    factor_of, own = 1.0, jax.random.fold_in(rng, 6)
    for axis_at, blocks in shards:
        steps = jnp.exp(jax.random.uniform(jax.random.fold_in(own, axis_at), (blocks,), jnp.float32, smallest / len(shards), largest / len(shards)))
        factor_of = factor_of * jnp.repeat(steps, extent[axis_at] // blocks).reshape([-1 if axis == axis_at else 1 for axis in range(len(extent))])
    return factor_of


def gaussian(rng, extent, scale, bound, cuts=(), kind=jnp.bfloat16):
    array = jax.random.normal(rng, extent, jnp.float32) * scale
    if len(cuts) > 0:
        array = block_scale(rng, extent, cuts, -0.22, 0.18) * array
    return jnp.clip(array, min=-bound, max=bound).astype(kind)


def setup_inputs(seed: int = 0, part: int = 0) -> dict:
    splits = jax.random.split(jax.random.key(seed), 12)
    part_splits = jax.random.split(jax.random.fold_in(splits[11], part), 12)
    return {
        "features": gaussian(part_splits[0], (FOLDS, WINDOWS, WE, WE, WE * CIN), 1.0, 6.0, ((0, 2), (1, 8))),
        "conv_first": gaussian(splits[1], (FOLDS, 3, 3, 3, CIN, CH), (27 * CIN) ** -0.5, 0.15625, ((0, 2),)),
        "gain_first": jnp.clip(1.0 + 0.18 * jax.random.normal(splits[2], (FOLDS, CH), jnp.float32), 0.1, 1.9),
        "shift_first": gaussian(splits[3], (FOLDS, CH), 0.5, 3.0, ((0, 2),), jnp.float32),
        "conv_second": gaussian(splits[4], (FOLDS, 3, 3, 3, CH, CH), (27 * CH) ** -0.5, 0.21875, ((0, 2),)),
        "gain_second": jnp.clip(1.0 + 0.18 * jax.random.normal(splits[5], (FOLDS, CH), jnp.float32), 0.1, 1.9),
        "shift_second": gaussian(splits[6], (FOLDS, CH), 0.5, 3.0, ((0, 2),), jnp.float32),
        "head_weight": gaussian(splits[7], (FOLDS, CH, CLASSES), CH ** -0.5, 1.0, ((0, 2),)),
        "head_bias": gaussian(splits[8], (FOLDS, CLASSES), 1.0, 4.0, ((0, 2),), jnp.float32),
        "corners": draw_corners(jax.random.fold_in(jax.random.fold_in(splits[11], part), 71), part),
        "counts": draw_counts(jax.random.fold_in(jax.random.fold_in(splits[11], part), 71), part),
    }


epsilon = 1e-05
leak_slope = 0.01

def gauss_table():
    coords = jnp.arange(WE, dtype=jnp.float32)
    center = (WE - 1) / 2.0
    spread = WE / 4.0
    profile = jnp.exp(-(coords - center) ** 2 / (2.0 * spread * spread))
    return profile[:, None, None] * profile[None, :, None] * profile[None, None, :]

def convolve(inputs, kernel):
    return lax.conv_general_dilated(inputs, kernel, (1, 1, 1), 'SAME', dimension_numbers=('NDHWC', 'DHWIO', 'NDHWC'), preferred_element_type=jnp.float32)

def normalize(hidden, gain_vec, shift_vec):
    mean_value = lax.optimization_barrier(jnp.mean(hidden, axis=(1, 2, 3), keepdims=True))
    variance = lax.optimization_barrier(jnp.mean((hidden - mean_value) ** 2, axis=(1, 2, 3), keepdims=True))
    scaled = (hidden - mean_value) * lax.rsqrt(variance + epsilon) * gain_vec + shift_vec
    return jnp.where(scaled >= 0, scaled, leak_slope * scaled).astype(jnp.bfloat16)

def decode(windows, kernel_one, gain_one, shift_one, kernel_two, gain_two, shift_two, head_kernel, head_shift):
    count = windows.shape[0]
    inputs = windows.reshape(count, WE, WE, WE, CIN)
    normed_first = normalize(convolve(inputs, kernel_one), gain_one, shift_one)
    normed_second = normalize(convolve(normed_first, kernel_two), gain_two, shift_two)
    head = jnp.einsum('nzxyc,ck->nzxyk', normed_second.astype(jnp.float32), head_kernel.astype(jnp.float32))
    weighted = ((head + head_shift) * gauss_table()[None, :, :, :, None]).astype(jnp.bfloat16)
    return weighted.reshape(count, WE, WE, WE * CLASSES)

def reference(features, conv_first, gain_first, shift_first, conv_second, gain_second, shift_second, head_weight, head_bias, corners, counts):
    volume = jnp.zeros((VZ + WE, VX, VY * CLASSES), jnp.float32)
    live_mask = (jnp.arange(CAP, dtype=jnp.int32)[None, None, :] < counts[:, :, None]).reshape(-1).astype(jnp.float32)
    for fold_index in range(FOLDS):
        weighted = decode(features[fold_index], conv_first[fold_index], gain_first[fold_index], shift_first[fold_index], conv_second[fold_index], gain_second[fold_index], shift_second[fold_index], head_weight[fold_index], head_bias[fold_index])

        def add_one(slot_index, total):
            window_piece = weighted[slot_index].astype(jnp.float32) * live_mask[slot_index]
            corner_start = (corners[slot_index, 0].astype(jnp.int32), corners[slot_index, 1].astype(jnp.int32), (corners[slot_index, 2] * CLASSES).astype(jnp.int32))
            current = lax.dynamic_slice(total, corner_start, window_piece.shape)
            return lax.dynamic_update_slice(total, current + window_piece, corner_start)
        volume = lax.fori_loop(0, WINDOWS, add_one, volume)
    return volume[:VZ]
```

```python
import functools

import jax
import jax.numpy as jnp
from jax import lax
from jax.experimental import pallas as pl
from jax.experimental.pallas import tpu as pltpu
from jax.sharding import PartitionSpec as P

CH = 32
CLASSES = 16
WE = 16
TZ = 16
VX = 40
VY = 40
ROWS = WE * WE
EXT = TZ + WE
LANES = WE * CLASSES + 128

epsilon = 1e-05
leak_slope = 0.01

f32 = jnp.float32
bf16 = jnp.bfloat16


def iota(shape, dim):
    return lax.broadcasted_iota(jnp.int32, shape, dim)


def one_hot(mask):
    return jnp.where(mask, 1.0, 0.0)


def exact_dot(a, b):
    return jnp.dot(a, b, precision=lax.Precision.HIGHEST, preferred_element_type=f32)


def spread_lanes(vec, width):
    n = vec.shape[1]
    pick = one_hot(iota((n, width), 0) == iota((n, width), 1) % n)
    return exact_dot(vec, pick)


def build_band(taps_ref, band, in_width, lead):
    pick = one_hot(iota((CH, 8 * CH), 0) == iota((CH, 8 * CH), 1) % CH).astype(bf16)
    band[...] = jnp.zeros_like(band)
    out_voxel = iota((in_width, 8 * CH), 1) // CH
    for dz in range(3):
        for dx in range(3):
            start = (dz * 3 + dx) * 3 * in_width
            spread = [
                jnp.dot(
                    taps_ref[start + dy * in_width : start + (dy + 1) * in_width, :],
                    pick,
                    preferred_element_type=f32,
                )
                for dy in range(3)
            ]
            for r in range(-1, 9):
                block = jnp.zeros((in_width, 8 * CH), f32)
                for dy in range(3):
                    if 0 <= r + 1 - dy < 8:
                        block = jnp.where(out_voxel == r + 1 - dy, spread[dy], block)
                band[
                    dz,
                    (r + lead) * in_width : (r + lead + 1) * in_width,
                    dx * 8 * CH : (dx + 1) * 8 * CH,
                ] = block.astype(bf16)


def convolve(padded, band, hidden, columns, band_rows):
    n = padded.shape[0]
    across = iota((n * ROWS, 8 * CH), 0) % WE
    for block in range(2):
        lo, width = columns[block]
        view = jnp.concatenate(
            [
                jnp.concatenate(
                    [padded[w, dz * WE : dz * WE + ROWS, lo : lo + width] for dz in range(3)],
                    axis=1,
                )
                for w in range(n)
            ],
            axis=0,
        )
        first = band_rows[block]
        weights = jnp.concatenate([band[dz, first : first + width, :] for dz in range(3)], axis=0)
        res = jnp.dot(view, weights, preferred_element_type=f32)
        before = pltpu.roll(res[:, : 8 * CH], 1, 0)
        after = pltpu.roll(res[:, 16 * CH :], n * ROWS - 1, 0)
        hidden[:, block * 8 * CH : (block + 1) * 8 * CH] = (
            res[:, 8 * CH : 16 * CH]
            + jnp.where(across == 0, 0.0, before)
            + jnp.where(across == WE - 1, 0.0, after)
        )


def group_sum(row):
    by = row.shape[1] // 2
    while by >= CH:
        row = row + pltpu.roll(row, by, 1)
        by //= 2
    return row


def normalize(hidden, gain, shift):
    voxels = float(WE * WE * WE)
    mean_value = group_sum(jnp.sum(hidden, axis=0, keepdims=True)) / voxels
    centered = hidden - mean_value
    variance = group_sum(jnp.sum(centered * centered, axis=0, keepdims=True)) / voxels
    scaled = centered * (lax.rsqrt(variance + epsilon) * gain) + shift
    return jnp.where(scaled >= 0, scaled, leak_slope * scaled).astype(bf16)


def decode_kernel(
    features,
    taps_first,
    gain_first,
    shift_first,
    taps_second,
    gain_second,
    shift_second,
    head_weight,
    head_bias,
    corners,
    counts,
    out,
    padded,
    normed,
    band_first,
    band_second,
    hidden,
    ext,
    sems,
):
    n = padded.shape[0]
    cin = padded.shape[2] // WE
    loads = [
        pltpu.make_async_copy(features.at[w], padded.at[w, WE : WE + ROWS, :], sems.at[w])
        for w in range(n)
    ]
    for load in loads:
        load.start()
    for w in range(n):
        padded[w, :WE, :] = jnp.zeros((WE, padded.shape[2]), bf16)
        padded[w, WE + ROWS :, :] = jnp.zeros((WE, padded.shape[2]), bf16)
        normed[w, :WE, :] = jnp.zeros((WE, normed.shape[2]), bf16)
        normed[w, WE + ROWS :, :] = jnp.zeros((WE, normed.shape[2]), bf16)
    ext[...] = jnp.zeros_like(ext)
    build_band(taps_first, band_first, cin, 4)
    build_band(taps_second, band_second, CH, 8)
    gains = [spread_lanes(g[...], WE * CH) for g in (gain_first, gain_second)]
    shifts = [spread_lanes(s[...], WE * CH) for s in (shift_first, shift_second)]
    for load in loads:
        load.wait()
    convolve(padded, band_first, hidden, ((0, 12 * cin), (4 * cin, 12 * cin)), (4 * cin, 0))
    for w in range(n):
        normed[w, WE : WE + ROWS, :] = normalize(
            hidden[w * ROWS : (w + 1) * ROWS, :], gains[0], shifts[0]
        )
    convolve(normed, band_second, hidden, ((0, 16 * CH), (0, 16 * CH)), (8 * CH, 0))

    tile = lax.axis_index("tiles")
    live_count = counts[tile, lax.axis_index("sub")]
    width = WE * CH
    pick_rows = one_hot(iota((width, CH), 0) % CH == iota((width, CH), 1)).astype(bf16)
    pick_lanes = one_hot(iota((CLASSES, LANES), 0) == iota((CLASSES, LANES), 1) % CLASSES)
    head_rows = jnp.dot(pick_rows, head_weight[...], preferred_element_type=f32).astype(bf16)
    head_full = jnp.dot(head_rows, pick_lanes.astype(bf16), preferred_element_type=f32)
    bias = spread_lanes(head_bias[...], LANES)
    head_gap = iota((width, LANES), 1) // CLASSES - iota((width, LANES), 0) // CH
    place_rows = iota((WE * EXT, ROWS), 0)
    place_cols = iota((WE * EXT, ROWS), 1)
    same_across = place_rows // EXT == place_cols % WE
    depth_gap = place_rows % EXT - place_cols // WE
    row_id = iota((WE * EXT, 1), 0)
    lane_id = iota((1, LANES), 1)
    center = (WE - 1) / 2.0
    spread = 2.0 * (WE / 4.0) ** 2
    for w in range(n):
        second = normalize(hidden[w * ROWS : (w + 1) * ROWS, :], gains[1], shifts[1])
        cz = corners[w, 0] - tile * TZ
        cx = corners[w, 1]
        cy = corners[w, 2]
        lane_tile = jnp.minimum(cy // 8, (VY - 24) // 8)
        rot = cy - lane_tile * 8
        placed = one_hot(same_across & (depth_gap == cz)).astype(bf16)
        moved = jnp.dot(placed, second, preferred_element_type=f32).astype(bf16)
        head = jnp.where(head_gap == rot, head_full, 0.0).astype(bf16)
        logits = jnp.dot(moved, head, preferred_element_type=f32) + bias
        z = row_id % EXT - cz
        across = (row_id // EXT).astype(f32) - center
        depth = z.astype(f32) - center
        gauss_rows = jnp.exp(-(depth * depth) / spread) * jnp.exp(-(across * across) / spread)
        gauss_rows = jnp.where((z >= 0) & (z < WE) & (w < live_count), gauss_rows, 0.0)
        y = lane_id // CLASSES - rot
        along = y.astype(f32) - center
        gauss_lanes = jnp.exp(-(along * along) / spread)
        gauss_lanes = jnp.where((y >= 0) & (y < WE), gauss_lanes, 0.0)
        weighted = (logits * (gauss_rows * gauss_lanes)).astype(bf16).astype(f32)
        lanes = pl.ds(pl.multiple_of(lane_tile * 128, 128), LANES)
        ext[pl.ds(cx, WE), :, lanes] += weighted.reshape(WE, EXT, LANES)
    out[...] = ext[...].astype(bf16)


def decode(features, taps_first, gf, sf, taps_second, gs, ss, hw, hb, corners, counts):
    n = features.shape[0]
    in_width = features.shape[-1]
    cin = in_width // WE
    vmem = pl.BlockSpec(memory_space=pltpu.VMEM)
    smem = pl.BlockSpec(memory_space=pltpu.SMEM)
    return pl.pallas_call(
        decode_kernel,
        out_shape=jax.ShapeDtypeStruct((VX, EXT, VY * CLASSES), bf16),
        in_specs=[pl.BlockSpec(memory_space=pl.ANY)] + [vmem] * 8 + [smem] * 2,
        out_specs=vmem,
        scratch_shapes=[
            pltpu.VMEM((n, ROWS + 2 * WE, in_width), bf16),
            pltpu.VMEM((n, ROWS + 2 * WE, WE * CH), bf16),
            pltpu.VMEM((3, 16 * cin, 24 * CH), bf16),
            pltpu.VMEM((3, 24 * CH, 24 * CH), bf16),
            pltpu.VMEM((n * ROWS, WE * CH), f32),
            pltpu.VMEM((VX, EXT, VY * CLASSES), f32),
            pltpu.SemaphoreType.DMA((n,)),
        ],
        compiler_params=pltpu.CompilerParams(vmem_limit_bytes=56 * 1024 * 1024),
    )(
        features.reshape(n, ROWS, in_width),
        taps_first.reshape(27 * cin, CH),
        gf,
        sf,
        taps_second.reshape(27 * CH, CH),
        gs,
        ss,
        hw,
        hb,
        corners,
        counts,
    )


def on_device(
    features,
    conv_first,
    gain_first,
    shift_first,
    conv_second,
    gain_second,
    shift_second,
    head_weight,
    head_bias,
    corners,
    counts,
):
    extended = decode(
        features[0],
        conv_first[0],
        gain_first,
        shift_first,
        conv_second[0],
        gain_second,
        shift_second,
        head_weight[0],
        head_bias,
        corners,
        counts,
    )
    shares = lax.psum_scatter(extended, ("folds", "sub"), scatter_dimension=0, tiled=True)
    length = lax.axis_size("tiles")
    pairs = [(i, i + 1) for i in range(length - 1)]
    arrived = lax.ppermute(shares[:, TZ:], "tiles", pairs)
    total = shares[:, :TZ].astype(f32) + arrived.astype(f32)
    return total.transpose(1, 0, 2)


def solution(mesh):
    placed = (
        P("folds", ("groups", "tiles", "sub"), None, None, None),
        P("folds", None, None, None, None, None),
        P("folds", None),
        P("folds", None),
        P("folds", None, None, None, None, None),
        P("folds", None),
        P("folds", None),
        P("folds", None, None),
        P("folds", None),
        P(("groups", "tiles", "sub"), None),
        P("groups", None),
    )
    return jax.shard_map(
        on_device,
        mesh=mesh,
        in_specs=placed,
        out_specs=P(("groups", "tiles"), ("folds", "sub"), None),
        check_vma=False,
    )
```

```python
import functools

import jax
import jax.numpy as jnp
from jax import lax
from jax.experimental import pallas as pl
from jax.experimental.pallas import tpu as pltpu
from jax.sharding import PartitionSpec as P

CH = 32
CLASSES = 16
WE = 16
TZ = 16
VX = 40
VY = 40
ROWS = WE * WE
EXT = TZ + WE
LANES = WE * CLASSES + 128

epsilon = 1e-05
leak_slope = 0.01

f32 = jnp.float32
bf16 = jnp.bfloat16


def iota(shape, dim):
    return lax.broadcasted_iota(jnp.int32, shape, dim)


def one_hot(mask):
    return jnp.where(mask, 1.0, 0.0)


def exact_dot(a, b):
    return jnp.dot(a, b, precision=lax.Precision.HIGHEST, preferred_element_type=f32)


def spread_lanes(vec, width):
    n = vec.shape[1]
    pick = one_hot(iota((n, width), 0) == iota((n, width), 1) % n)
    return exact_dot(vec, pick)


def build_band(taps_ref, band, in_width, lead):
    pick = one_hot(iota((CH, 8 * CH), 0) == iota((CH, 8 * CH), 1) % CH).astype(bf16)
    band[...] = jnp.zeros_like(band)
    out_voxel = iota((in_width, 8 * CH), 1) // CH
    for dz in range(3):
        for dx in range(3):
            start = (dz * 3 + dx) * 3 * in_width
            spread = [
                jnp.dot(
                    taps_ref[start + dy * in_width : start + (dy + 1) * in_width, :],
                    pick,
                    preferred_element_type=f32,
                )
                for dy in range(3)
            ]
            for r in range(-1, 9):
                block = jnp.zeros((in_width, 8 * CH), f32)
                for dy in range(3):
                    if 0 <= r + 1 - dy < 8:
                        block = jnp.where(out_voxel == r + 1 - dy, spread[dy], block)
                band[
                    dz,
                    (r + lead) * in_width : (r + lead + 1) * in_width,
                    dx * 8 * CH : (dx + 1) * 8 * CH,
                ] = block.astype(bf16)


def convolve(padded, band, hidden, columns, band_rows):
    n = padded.shape[0]
    across = iota((n * ROWS, 8 * CH), 0) % WE
    for block in range(2):
        lo, width = columns[block]
        view = jnp.concatenate(
            [
                jnp.concatenate(
                    [padded[w, dz * WE : dz * WE + ROWS, lo : lo + width] for dz in range(3)],
                    axis=1,
                )
                for w in range(n)
            ],
            axis=0,
        )
        first = band_rows[block]
        weights = jnp.concatenate([band[dz, first : first + width, :] for dz in range(3)], axis=0)
        res = jnp.dot(view, weights, preferred_element_type=f32)
        before = pltpu.roll(res[:, : 8 * CH], 1, 0)
        after = pltpu.roll(res[:, 16 * CH :], n * ROWS - 1, 0)
        hidden[:, block * 8 * CH : (block + 1) * 8 * CH] = (
            res[:, 8 * CH : 16 * CH]
            + jnp.where(across == 0, 0.0, before)
            + jnp.where(across == WE - 1, 0.0, after)
        )


def group_sum(row):
    by = row.shape[1] // 2
    while by >= CH:
        row = row + pltpu.roll(row, by, 1)
        by //= 2
    return row


def normalize(hidden, gain, shift):
    voxels = float(WE * WE * WE)
    mean_value = group_sum(jnp.sum(hidden, axis=0, keepdims=True)) / voxels
    centered = hidden - mean_value
    variance = group_sum(jnp.sum(centered * centered, axis=0, keepdims=True)) / voxels
    scaled = centered * (lax.rsqrt(variance + epsilon) * gain) + shift
    return jnp.where(scaled >= 0, scaled, leak_slope * scaled).astype(bf16)


def decode_kernel(
    features,
    taps_first,
    gain_first,
    shift_first,
    taps_second,
    gain_second,
    shift_second,
    head_weight,
    head_bias,
    corners,
    counts,
    out,
    padded,
    normed,
    band_first,
    band_second,
    hidden,
    ext,
    sems,
):
    n = padded.shape[0]
    cin = padded.shape[2] // WE
    loads = [
        pltpu.make_async_copy(features.at[w], padded.at[w, WE : WE + ROWS, :], sems.at[w])
        for w in range(n)
    ]
    for load in loads:
        load.start()
    for w in range(n):
        padded[w, :WE, :] = jnp.zeros((WE, padded.shape[2]), bf16)
        padded[w, WE + ROWS :, :] = jnp.zeros((WE, padded.shape[2]), bf16)
        normed[w, :WE, :] = jnp.zeros((WE, normed.shape[2]), bf16)
        normed[w, WE + ROWS :, :] = jnp.zeros((WE, normed.shape[2]), bf16)
    ext[...] = jnp.zeros_like(ext)
    build_band(taps_first, band_first, cin, 4)
    build_band(taps_second, band_second, CH, 8)
    gains = [spread_lanes(g[...], WE * CH) for g in (gain_first, gain_second)]
    shifts = [spread_lanes(s[...], WE * CH) for s in (shift_first, shift_second)]
    for load in loads:
        load.wait()
    convolve(padded, band_first, hidden, ((0, 12 * cin), (4 * cin, 12 * cin)), (4 * cin, 0))
    for w in range(n):
        normed[w, WE : WE + ROWS, :] = normalize(
            hidden[w * ROWS : (w + 1) * ROWS, :], gains[0], shifts[0]
        )
    convolve(normed, band_second, hidden, ((0, 16 * CH), (0, 16 * CH)), (8 * CH, 0))

    tile = lax.axis_index("tiles")
    live_count = counts[tile, lax.axis_index("sub")]
    width = WE * CH
    pick_rows = one_hot(iota((width, CH), 0) % CH == iota((width, CH), 1)).astype(bf16)
    pick_lanes = one_hot(iota((CLASSES, LANES), 0) == iota((CLASSES, LANES), 1) % CLASSES)
    head_rows = jnp.dot(pick_rows, head_weight[...], preferred_element_type=f32).astype(bf16)
    head_full = jnp.dot(head_rows, pick_lanes.astype(bf16), preferred_element_type=f32)
    bias = spread_lanes(head_bias[...], LANES)
    head_gap = iota((width, LANES), 1) // CLASSES - iota((width, LANES), 0) // CH
    place_rows = iota((WE * EXT, ROWS), 0)
    place_cols = iota((WE * EXT, ROWS), 1)
    same_across = place_rows // EXT == place_cols % WE
    depth_gap = place_rows % EXT - place_cols // WE
    row_id = iota((WE * EXT, 1), 0)
    lane_id = iota((1, LANES), 1)
    center = (WE - 1) / 2.0
    spread = 2.0 * (WE / 4.0) ** 2
    for w in range(n):
        second = normalize(hidden[w * ROWS : (w + 1) * ROWS, :], gains[1], shifts[1])
        cz = corners[w, 0] - tile * TZ
        cx = corners[w, 1]
        cy = corners[w, 2]
        lane_tile = jnp.minimum(cy // 8, (VY - 24) // 8)
        rot = cy - lane_tile * 8
        placed = one_hot(same_across & (depth_gap == cz)).astype(bf16)
        moved = jnp.dot(placed, second, preferred_element_type=f32).astype(bf16)
        head = jnp.where(head_gap == rot, head_full, 0.0).astype(bf16)
        logits = jnp.dot(moved, head, preferred_element_type=f32) + bias
        z = row_id % EXT - cz
        across = (row_id // EXT).astype(f32) - center
        depth = z.astype(f32) - center
        gauss_rows = jnp.exp(-(depth * depth) / spread) * jnp.exp(-(across * across) / spread)
        gauss_rows = jnp.where((z >= 0) & (z < WE) & (w < live_count), gauss_rows, 0.0)
        y = lane_id // CLASSES - rot
        along = y.astype(f32) - center
        gauss_lanes = jnp.exp(-(along * along) / spread)
        gauss_lanes = jnp.where((y >= 0) & (y < WE), gauss_lanes, 0.0)
        weighted = (logits * (gauss_rows * gauss_lanes)).astype(bf16).astype(f32)
        lanes = pl.ds(pl.multiple_of(lane_tile * 128, 128), LANES)
        ext[pl.ds(cx, WE), :, lanes] += weighted.reshape(WE, EXT, LANES)
    out[...] = ext[...].astype(bf16)


def decode(features, taps_first, gf, sf, taps_second, gs, ss, hw, hb, corners, counts):
    n = features.shape[0]
    in_width = features.shape[-1]
    cin = in_width // WE
    vmem = pl.BlockSpec(memory_space=pltpu.VMEM)
    smem = pl.BlockSpec(memory_space=pltpu.SMEM)
    return pl.pallas_call(
        decode_kernel,
        out_shape=jax.ShapeDtypeStruct((VX, EXT, VY * CLASSES), bf16),
        in_specs=[pl.BlockSpec(memory_space=pl.ANY)] + [vmem] * 8 + [smem] * 2,
        out_specs=vmem,
        scratch_shapes=[
            pltpu.VMEM((n, ROWS + 2 * WE, in_width), bf16),
            pltpu.VMEM((n, ROWS + 2 * WE, WE * CH), bf16),
            pltpu.VMEM((3, 16 * cin, 24 * CH), bf16),
            pltpu.VMEM((3, 24 * CH, 24 * CH), bf16),
            pltpu.VMEM((n * ROWS, WE * CH), f32),
            pltpu.VMEM((VX, EXT, VY * CLASSES), f32),
            pltpu.SemaphoreType.DMA((n,)),
        ],
        compiler_params=pltpu.CompilerParams(vmem_limit_bytes=56 * 1024 * 1024),
    )(
        features.reshape(n, ROWS, in_width),
        taps_first.reshape(27 * cin, CH),
        gf,
        sf,
        taps_second.reshape(27 * CH, CH),
        gs,
        ss,
        hw,
        hb,
        corners,
        counts,
    )


def exchange_kernel(
    ext,
    out,
    got_sub,
    part,
    got_fold,
    tail,
    got_tail,
    sub_send,
    sub_recv,
    fold_send,
    fold_recv,
    tile_send,
    tile_recv,
):
    fold, sub, tile = (lax.axis_index(a) for a in ("folds", "sub", "tiles"))
    folds, subs, tiles = (lax.axis_size(a) for a in ("folds", "sub", "tiles"))
    span = out.shape[0]
    chunks = 2 if span % 2 == 0 else 1
    step = span // chunks
    mesh_id = pl.DeviceIdType.MESH
    barrier = pltpu.get_barrier_semaphore()

    def greet(where):
        pl.semaphore_signal(barrier, inc=1, device_id=where, device_id_type=mesh_id)

    for e in range(1, subs):
        greet({"sub": lax.rem(sub + e, subs)})
    for d in range(1, folds):
        greet({"folds": lax.rem(fold + d, folds)})

    @pl.when(tile < tiles - 1)
    def _():
        greet({"tiles": tile + 1})

    @pl.when(tile > 0)
    def _():
        greet({"tiles": tile - 1})

    peers = subs - 1 + folds - 1
    at_end = (tile == 0) | (tile == tiles - 1)

    @pl.when(at_end)
    def _():
        pl.semaphore_wait(barrier, peers + 1)

    @pl.when(jnp.logical_not(at_end))
    def _():
        pl.semaphore_wait(barrier, peers + 2)

    def own(d, of_sub, half, k):
        first = (lax.rem(fold + d, folds) * subs + of_sub) * span + k * step
        return ext.at[pl.ds(first, step), pl.ds(half * TZ, TZ), :]

    def rows(k):
        return pl.ds(k * step, step)

    order = list(range(1, folds)) + [0]
    to_sub = {}
    for group in (order[:-1], order[-1:]):
        for half in (1, 0):
            for d in group:
                for k in range(chunks):
                    for e in range(1, subs):
                        peer = lax.rem(sub + e, subs)
                        copy = pltpu.make_async_remote_copy(
                            src_ref=own(d, peer, half, k),
                            dst_ref=got_sub.at[e - 1, d, half, rows(k)],
                            send_sem=sub_send.at[e - 1, d, half, k],
                            recv_sem=sub_recv.at[e - 1, d, half, k],
                            device_id={"sub": peer},
                            device_id_type=mesh_id,
                        )
                        copy.start()
                        to_sub[e, d, half, k] = copy

    def chip_sum(d, half, k):
        total = own(d, sub, half, k)[...].astype(f32)
        for e in range(1, subs):
            to_sub[e, d, half, k].wait_recv()
            total = total + got_sub[e - 1, d, half, rows(k)].astype(f32)
        return total

    to_fold = {}
    for half in (1, 0):
        for d in range(1, folds):
            for k in range(chunks):
                part[d - 1, half, rows(k)] = chip_sum(d, half, k).astype(bf16)
                copy = pltpu.make_async_remote_copy(
                    src_ref=part.at[d - 1, half, rows(k)],
                    dst_ref=got_fold.at[d - 1, half, rows(k)],
                    send_sem=fold_send.at[d - 1, half, k],
                    recv_sem=fold_recv.at[d - 1, half, k],
                    device_id={"folds": lax.rem(fold + d, folds)},
                    device_id_type=mesh_id,
                )
                copy.start()
                to_fold[d, half, k] = copy

    def full_sum(half, k):
        total = chip_sum(0, half, k)
        for d in range(1, folds):
            to_fold[d, half, k].wait_recv()
            total = total + got_fold[d - 1, half, rows(k)].astype(f32)
        return total

    to_tile = [
        pltpu.make_async_remote_copy(
            src_ref=tail.at[rows(k)],
            dst_ref=got_tail.at[rows(k)],
            send_sem=tile_send.at[k],
            recv_sem=tile_recv.at[k],
            device_id={"tiles": lax.rem(tile + 1, tiles)},
            device_id_type=mesh_id,
        )
        for k in range(chunks)
    ]
    for k in range(chunks):
        tail[rows(k)] = full_sum(1, k).astype(bf16)

        @pl.when(tile < tiles - 1)
        def _():
            to_tile[k].start()

    for k in range(chunks):
        out[rows(k)] = full_sum(0, k)

    @pl.when(tile > 0)
    def _():
        for k in range(chunks):
            to_tile[k].wait_recv()
            out[rows(k)] += got_tail[rows(k)].astype(f32)

    for copy in list(to_sub.values()) + list(to_fold.values()):
        copy.wait_send()

    @pl.when(tile < tiles - 1)
    def _():
        for copy in to_tile:
            copy.wait_send()


def exchange(ext):
    folds, subs = lax.axis_size("folds"), lax.axis_size("sub")
    span = VX // (folds * subs)
    lanes = VY * CLASSES
    chunks = 2 if span % 2 == 0 else 1
    vmem = pl.BlockSpec(memory_space=pltpu.VMEM)
    dma = pltpu.SemaphoreType.DMA
    return pl.pallas_call(
        exchange_kernel,
        out_shape=jax.ShapeDtypeStruct((span, TZ, lanes), f32),
        in_specs=[vmem],
        out_specs=vmem,
        scratch_shapes=[
            pltpu.VMEM((subs - 1, folds, 2, span, TZ, lanes), bf16),
            pltpu.VMEM((folds - 1, 2, span, TZ, lanes), bf16),
            pltpu.VMEM((folds - 1, 2, span, TZ, lanes), bf16),
            pltpu.VMEM((span, TZ, lanes), bf16),
            pltpu.VMEM((span, TZ, lanes), bf16),
            dma((subs - 1, folds, 2, chunks)),
            dma((subs - 1, folds, 2, chunks)),
            dma((folds - 1, 2, chunks)),
            dma((folds - 1, 2, chunks)),
            dma((chunks,)),
            dma((chunks,)),
        ],
        compiler_params=pltpu.CompilerParams(
            collective_id=0, has_side_effects=True, vmem_limit_bytes=32 * 1024 * 1024
        ),
    )(ext)


def on_device(
    features,
    conv_first,
    gain_first,
    shift_first,
    conv_second,
    gain_second,
    shift_second,
    head_weight,
    head_bias,
    corners,
    counts,
):
    extended = decode(
        features[0],
        conv_first[0],
        gain_first,
        shift_first,
        conv_second[0],
        gain_second,
        shift_second,
        head_weight[0],
        head_bias,
        corners,
        counts,
    )
    return exchange(extended).transpose(1, 0, 2)


def solution(mesh):
    placed = (
        P("folds", ("groups", "tiles", "sub"), None, None, None),
        P("folds", None, None, None, None, None),
        P("folds", None),
        P("folds", None),
        P("folds", None, None, None, None, None),
        P("folds", None),
        P("folds", None),
        P("folds", None, None),
        P("folds", None),
        P(("groups", "tiles", "sub"), None),
        P("groups", None),
    )
    return jax.shard_map(
        on_device,
        mesh=mesh,
        in_specs=placed,
        out_specs=P(("groups", "tiles"), ("folds", "sub"), None),
        check_vma=False,
    )
```

```python
import functools

import jax
import jax.numpy as jnp
from jax import lax
from jax.experimental import pallas as pl
from jax.experimental.pallas import tpu as pltpu
from jax.sharding import PartitionSpec as P

CH = 32
CLASSES = 16
WE = 16
TZ = 16
VX = 40
VY = 40
ROWS = WE * WE
EXT = TZ + WE
LANES = WE * CLASSES + 128

epsilon = 1e-05
leak_slope = 0.01

f32 = jnp.float32
bf16 = jnp.bfloat16


def iota(shape, dim):
    return lax.broadcasted_iota(jnp.int32, shape, dim)


def one_hot(mask):
    return jnp.where(mask, 1.0, 0.0)


def exact_dot(a, b):
    return jnp.dot(a, b, precision=lax.Precision.HIGHEST, preferred_element_type=f32)


def spread_lanes(vec, width):
    n = vec.shape[1]
    pick = one_hot(iota((n, width), 0) == iota((n, width), 1) % n)
    return exact_dot(vec, pick)


def build_band(taps_ref, band, in_width, lead, flipped):
    pick = one_hot(iota((CH, 8 * CH), 0) == iota((CH, 8 * CH), 1) % CH).astype(bf16)
    written = ((lead - 1) * in_width, (lead + 9) * in_width)
    for lo, hi in ((0, written[0]), (written[1], band.shape[1])):
        band[:, lo:hi, :] = jnp.zeros((3, hi - lo, band.shape[2]), bf16)
    out_voxel = iota((in_width, 8 * CH), 1) // CH
    for dz in range(3):
        for dx in range(3):
            start = (dz * 3 + dx) * 3
            rows = CH if flipped else in_width
            spread = [
                lax.dot_general(
                    taps_ref[(start + dy) * rows : (start + dy + 1) * rows, :],
                    pick,
                    (((0 if flipped else 1,), (0,)), ((), ())),
                    preferred_element_type=f32,
                )
                for dy in range(3)
            ]
            for r in range(-1, 9):
                block = jnp.zeros((in_width, 8 * CH), f32)
                for dy in range(3):
                    if 0 <= r + 1 - dy < 8:
                        block = jnp.where(out_voxel == r + 1 - dy, spread[dy], block)
                band[
                    dz,
                    (r + lead) * in_width : (r + lead + 1) * in_width,
                    dx * 8 * CH : (dx + 1) * 8 * CH,
                ] = block.astype(bf16)


def convolve(padded, band, hidden, columns, band_rows):
    n = padded.shape[0]
    across = iota((n * ROWS, 8 * CH), 0) % WE
    for block in range(2):
        lo, width = columns[block]
        view = jnp.concatenate(
            [
                jnp.concatenate(
                    [padded[w, dz * WE : dz * WE + ROWS, lo : lo + width] for dz in range(3)],
                    axis=1,
                )
                for w in range(n)
            ],
            axis=0,
        )
        first = band_rows[block]
        weights = jnp.concatenate([band[dz, first : first + width, :] for dz in range(3)], axis=0)
        res = jnp.dot(view, weights, preferred_element_type=f32)
        before = pltpu.roll(res[:, : 8 * CH], 1, 0)
        after = pltpu.roll(res[:, 16 * CH :], n * ROWS - 1, 0)
        hidden[:, block * 8 * CH : (block + 1) * 8 * CH] = (
            res[:, 8 * CH : 16 * CH]
            + jnp.where(across == 0, 0.0, before)
            + jnp.where(across == WE - 1, 0.0, after)
        )


def group_sum(row):
    by = row.shape[1] // 2
    while by >= CH:
        row = row + pltpu.roll(row, by, 1)
        by //= 2
    return row


def normalize(hidden, gain, shift):
    voxels = float(WE * WE * WE)
    mean_value = group_sum(jnp.sum(hidden, axis=0, keepdims=True)) / voxels
    centered = hidden - mean_value
    variance = group_sum(jnp.sum(centered * centered, axis=0, keepdims=True)) / voxels
    scaled = centered * (lax.rsqrt(variance + epsilon) * gain) + shift
    return jnp.where(scaled >= 0, scaled, leak_slope * scaled).astype(bf16)


def decode_kernel(
    features,
    taps_first,
    gain_first,
    shift_first,
    taps_second,
    gain_second,
    shift_second,
    head_weight,
    head_bias,
    corners,
    counts,
    out,
    padded,
    normed,
    band_first,
    band_second,
    hidden,
    ext,
    sems,
):
    n = padded.shape[0]
    cin = padded.shape[2] // WE
    loads = [
        pltpu.make_async_copy(features.at[w], padded.at[w, WE : WE + ROWS, :], sems.at[w])
        for w in range(n)
    ]
    for load in loads:
        load.start()
    for w in range(n):
        padded[w, :WE, :] = jnp.zeros((WE, padded.shape[2]), bf16)
        padded[w, WE + ROWS :, :] = jnp.zeros((WE, padded.shape[2]), bf16)
        normed[w, :WE, :] = jnp.zeros((WE, normed.shape[2]), bf16)
        normed[w, WE + ROWS :, :] = jnp.zeros((WE, normed.shape[2]), bf16)
    ext[...] = jnp.zeros_like(ext)
    build_band(taps_first, band_first, cin, 2, True)
    build_band(taps_second, band_second, CH, 4, False)
    gains = [spread_lanes(g[...], WE * CH) for g in (gain_first, gain_second)]
    shifts = [spread_lanes(s[...], WE * CH) for s in (shift_first, shift_second)]
    for load in loads:
        load.wait()
    convolve(padded, band_first, hidden, ((0, 10 * cin), (6 * cin, 10 * cin)), (2 * cin, 0))
    for w in range(n):
        normed[w, WE : WE + ROWS, :] = normalize(
            hidden[w * ROWS : (w + 1) * ROWS, :], gains[0], shifts[0]
        )
    convolve(normed, band_second, hidden, ((0, 12 * CH), (4 * CH, 12 * CH)), (4 * CH, 0))

    tile = lax.axis_index("tiles")
    live_count = counts[lax.axis_index("sub"), tile]
    width = WE * CH
    pick_rows = one_hot(iota((width, CH), 0) % CH == iota((width, CH), 1)).astype(bf16)
    pick_lanes = one_hot(iota((CLASSES, LANES), 0) == iota((CLASSES, LANES), 1) % CLASSES)
    head_rows = lax.dot_general(
        pick_rows, head_weight[...], (((1,), (1,)), ((), ())), preferred_element_type=f32
    ).astype(bf16)
    head_full = jnp.dot(head_rows, pick_lanes.astype(bf16), preferred_element_type=f32)
    bias = spread_lanes(head_bias[...], LANES)
    head_gap = iota((width, LANES), 1) // CLASSES - iota((width, LANES), 0) // CH
    place_rows = iota((WE * EXT, ROWS), 0)
    place_cols = iota((WE * EXT, ROWS), 1)
    same_across = place_rows // EXT == place_cols % WE
    depth_gap = place_rows % EXT - place_cols // WE
    row_id = iota((WE * EXT, 1), 0)
    lane_id = iota((1, LANES), 1)
    center = (WE - 1) / 2.0
    spread = 2.0 * (WE / 4.0) ** 2
    for w in range(n):
        second = normalize(hidden[w * ROWS : (w + 1) * ROWS, :], gains[1], shifts[1])
        cz = corners[w, 0] - tile * TZ
        cx = corners[w, 1]
        cy = corners[w, 2]
        lane_tile = jnp.minimum(cy // 8, (VY - 24) // 8)
        rot = cy - lane_tile * 8
        placed = one_hot(same_across & (depth_gap == cz)).astype(bf16)
        moved = jnp.dot(placed, second, preferred_element_type=f32).astype(bf16)
        head = jnp.where(head_gap == rot, head_full, 0.0).astype(bf16)
        logits = jnp.dot(moved, head, preferred_element_type=f32) + bias
        z = row_id % EXT - cz
        across = (row_id // EXT).astype(f32) - center
        depth = z.astype(f32) - center
        gauss_rows = jnp.exp(-(depth * depth) / spread) * jnp.exp(-(across * across) / spread)
        gauss_rows = jnp.where((z >= 0) & (z < WE) & (w < live_count), gauss_rows, 0.0)
        y = lane_id // CLASSES - rot
        along = y.astype(f32) - center
        gauss_lanes = jnp.exp(-(along * along) / spread)
        gauss_lanes = jnp.where((y >= 0) & (y < WE), gauss_lanes, 0.0)
        weighted = (logits * (gauss_rows * gauss_lanes)).astype(bf16).astype(f32)
        lanes = pl.ds(pl.multiple_of(lane_tile * 128, 128), LANES)
        ext[pl.ds(cx, WE), :, lanes] += weighted.reshape(WE, EXT, LANES)
    out[...] = ext[...].astype(bf16)


def decode(features, taps_first, gf, sf, taps_second, gs, ss, hw, hb, corners, counts):
    n = features.shape[0]
    in_width = features.shape[-1]
    cin = in_width // WE
    vmem = pl.BlockSpec(memory_space=pltpu.VMEM)
    smem = pl.BlockSpec(memory_space=pltpu.SMEM)
    return pl.pallas_call(
        decode_kernel,
        out_shape=jax.ShapeDtypeStruct((VX, EXT, VY * CLASSES), bf16),
        in_specs=[pl.BlockSpec(memory_space=pltpu.HBM)] + [vmem] * 8 + [smem] * 2,
        out_specs=vmem,
        scratch_shapes=[
            pltpu.VMEM((n, ROWS + 2 * WE, in_width), bf16),
            pltpu.VMEM((n, ROWS + 2 * WE, WE * CH), bf16),
            pltpu.VMEM((3, 12 * cin, 24 * CH), bf16),
            pltpu.VMEM((3, 16 * CH, 24 * CH), bf16),
            pltpu.VMEM((n * ROWS, WE * CH), f32),
            pltpu.VMEM((VX, EXT, VY * CLASSES), f32),
            pltpu.SemaphoreType.DMA((n,)),
        ],
        compiler_params=pltpu.CompilerParams(vmem_limit_bytes=28 * 1024 * 1024),
    )(
        features.reshape(n, ROWS, in_width),
        taps_first.swapaxes(-1, -2).reshape(27 * CH, cin),
        gf,
        sf,
        taps_second.reshape(27 * CH, CH),
        gs,
        ss,
        hw.T,
        hb,
        corners,
        counts.T,
    )


def exchange_kernel(
    ext,
    out,
    got_sub,
    part,
    got_fold,
    tail,
    got_tail,
    sub_send,
    sub_recv,
    fold_send,
    fold_recv,
    tile_send,
    tile_recv,
):
    fold, sub, tile = (lax.axis_index(a) for a in ("folds", "sub", "tiles"))
    folds, subs, tiles = (lax.axis_size(a) for a in ("folds", "sub", "tiles"))
    span = out.shape[0]
    chunks = 2 if span % 2 == 0 else 1
    step = span // chunks
    mesh_id = pl.DeviceIdType.MESH
    barrier = pltpu.get_barrier_semaphore()

    def greet(where):
        pl.semaphore_signal(barrier, inc=1, device_id=where, device_id_type=mesh_id)

    for e in range(1, subs):
        greet({"sub": lax.rem(sub + e, subs)})
    for d in range(1, folds):
        greet({"folds": lax.rem(fold + d, folds)})

    @pl.when(tile < tiles - 1)
    def _():
        greet({"tiles": tile + 1})

    @pl.when(tile > 0)
    def _():
        greet({"tiles": tile - 1})

    peers = subs - 1 + folds - 1
    at_end = (tile == 0) | (tile == tiles - 1)

    @pl.when(at_end)
    def _():
        pl.semaphore_wait(barrier, peers + 1)

    @pl.when(jnp.logical_not(at_end))
    def _():
        pl.semaphore_wait(barrier, peers + 2)

    def own(d, of_sub, half, k):
        first = (lax.rem(fold + d, folds) * subs + of_sub) * span + k * step
        return ext.at[pl.ds(first, step), pl.ds(half * TZ, TZ), :]

    def rows(k):
        return pl.ds(k * step, step)

    order = list(range(1, folds)) + [0]
    to_sub = {}
    for group in (order[:-1], order[-1:]):
        for half in (1, 0):
            for d in group:
                for k in range(chunks):
                    for e in range(1, subs):
                        peer = lax.rem(sub + e, subs)
                        copy = pltpu.make_async_remote_copy(
                            src_ref=own(d, peer, half, k),
                            dst_ref=got_sub.at[e - 1, d, half, rows(k)],
                            send_sem=sub_send.at[e - 1, d, half, k],
                            recv_sem=sub_recv.at[e - 1, d, half, k],
                            device_id={"sub": peer},
                            device_id_type=mesh_id,
                        )
                        copy.start()
                        to_sub[e, d, half, k] = copy

    def chip_sum(d, half, k):
        total = own(d, sub, half, k)[...].astype(f32)
        for e in range(1, subs):
            to_sub[e, d, half, k].wait_recv()
            total = total + got_sub[e - 1, d, half, rows(k)].astype(f32)
        return total

    to_fold = {}
    for half in (1, 0):
        for d in range(1, folds):
            for k in range(chunks):
                part[d - 1, half, rows(k)] = chip_sum(d, half, k).astype(bf16)
                copy = pltpu.make_async_remote_copy(
                    src_ref=part.at[d - 1, half, rows(k)],
                    dst_ref=got_fold.at[d - 1, half, rows(k)],
                    send_sem=fold_send.at[d - 1, half, k],
                    recv_sem=fold_recv.at[d - 1, half, k],
                    device_id={"folds": lax.rem(fold + d, folds)},
                    device_id_type=mesh_id,
                )
                copy.start()
                to_fold[d, half, k] = copy

    def full_sum(half, k):
        total = chip_sum(0, half, k)
        for d in range(1, folds):
            to_fold[d, half, k].wait_recv()
            total = total + got_fold[d - 1, half, rows(k)].astype(f32)
        return total

    to_tile = [
        pltpu.make_async_remote_copy(
            src_ref=tail.at[rows(k)],
            dst_ref=got_tail.at[rows(k)],
            send_sem=tile_send.at[k],
            recv_sem=tile_recv.at[k],
            device_id={"tiles": lax.rem(tile + 1, tiles)},
            device_id_type=mesh_id,
        )
        for k in range(chunks)
    ]
    for k in range(chunks):
        tail[rows(k)] = full_sum(1, k).astype(bf16)

        @pl.when(tile < tiles - 1)
        def _():
            to_tile[k].start()

    for k in range(chunks):
        out[rows(k)] = full_sum(0, k)

    @pl.when(tile > 0)
    def _():
        for k in range(chunks):
            to_tile[k].wait_recv()
            out[rows(k)] += got_tail[rows(k)].astype(f32)

    for copy in list(to_sub.values()) + list(to_fold.values()):
        copy.wait_send()

    @pl.when(tile < tiles - 1)
    def _():
        for copy in to_tile:
            copy.wait_send()


def exchange(ext):
    folds, subs = lax.axis_size("folds"), lax.axis_size("sub")
    span = VX // (folds * subs)
    lanes = VY * CLASSES
    chunks = 2 if span % 2 == 0 else 1
    vmem = pl.BlockSpec(memory_space=pltpu.VMEM)
    dma = pltpu.SemaphoreType.DMA
    return pl.pallas_call(
        exchange_kernel,
        out_shape=jax.ShapeDtypeStruct((span, TZ, lanes), f32),
        in_specs=[vmem],
        out_specs=vmem,
        scratch_shapes=[
            pltpu.VMEM((subs - 1, folds, 2, span, TZ, lanes), bf16),
            pltpu.VMEM((folds - 1, 2, span, TZ, lanes), bf16),
            pltpu.VMEM((folds - 1, 2, span, TZ, lanes), bf16),
            pltpu.VMEM((span, TZ, lanes), bf16),
            pltpu.VMEM((span, TZ, lanes), bf16),
            dma((subs - 1, folds, 2, chunks)),
            dma((subs - 1, folds, 2, chunks)),
            dma((folds - 1, 2, chunks)),
            dma((folds - 1, 2, chunks)),
            dma((chunks,)),
            dma((chunks,)),
        ],
        compiler_params=pltpu.CompilerParams(
            collective_id=0, has_side_effects=True, vmem_limit_bytes=12 * 1024 * 1024
        ),
    )(ext)


def on_device(
    features,
    conv_first,
    gain_first,
    shift_first,
    conv_second,
    gain_second,
    shift_second,
    head_weight,
    head_bias,
    corners,
    counts,
):
    extended = decode(
        features[0],
        conv_first[0],
        gain_first,
        shift_first,
        conv_second[0],
        gain_second,
        shift_second,
        head_weight[0],
        head_bias,
        corners,
        counts,
    )
    return exchange(extended).transpose(1, 0, 2)


def solution(mesh):
    placed = (
        P("folds", ("groups", "tiles", "sub"), None, None, None),
        P("folds", None, None, None, None, None),
        P("folds", None),
        P("folds", None),
        P("folds", None, None, None, None, None),
        P("folds", None),
        P("folds", None),
        P("folds", None, None),
        P("folds", None),
        P(("groups", "tiles", "sub"), None),
        P("groups", None),
    )
    return jax.shard_map(
        on_device,
        mesh=mesh,
        in_specs=placed,
        out_specs=P(("groups", "tiles"), ("folds", "sub"), None),
        check_vma=False,
    )
```

```python
import functools

import jax
import jax.numpy as jnp
from jax import lax
from jax.experimental import pallas as pl
from jax.experimental.pallas import tpu as pltpu
from jax.sharding import PartitionSpec as P

CH = 32
CLASSES = 16
WE = 16
TZ = 16
VX = 40
VY = 40
ROWS = WE * WE
EXT = TZ + WE
LANES = WE * CLASSES + 128

epsilon = 1e-05
leak_slope = 0.01

f32 = jnp.float32
bf16 = jnp.bfloat16


def iota(shape, dim):
    return lax.broadcasted_iota(jnp.int32, shape, dim)


def one_hot(mask):
    return jnp.where(mask, 1.0, 0.0)


def exact_dot(a, b):
    return jnp.dot(a, b, precision=lax.Precision.HIGHEST, preferred_element_type=f32)


def spread_lanes(vec, width):
    n = vec.shape[1]
    pick = one_hot(iota((n, width), 0) == iota((n, width), 1) % n)
    return exact_dot(vec, pick)


def build_band(taps_ref, band, in_width, lead, flipped):
    pick = one_hot(iota((CH, 8 * CH), 0) == iota((CH, 8 * CH), 1) % CH).astype(bf16)
    written = ((lead - 1) * in_width, (lead + 9) * in_width)
    for lo, hi in ((0, written[0]), (written[1], band.shape[1])):
        band[:, lo:hi, :] = jnp.zeros((3, hi - lo, band.shape[2]), bf16)
    out_voxel = iota((in_width, 8 * CH), 1) // CH
    for dz in range(3):
        for dx in range(3):
            start = (dz * 3 + dx) * 3
            rows = CH if flipped else in_width
            spread = [
                lax.dot_general(
                    taps_ref[(start + dy) * rows : (start + dy + 1) * rows, :],
                    pick,
                    (((0 if flipped else 1,), (0,)), ((), ())),
                    preferred_element_type=f32,
                )
                for dy in range(3)
            ]
            for r in range(-1, 9):
                block = jnp.zeros((in_width, 8 * CH), f32)
                for dy in range(3):
                    if 0 <= r + 1 - dy < 8:
                        block = jnp.where(out_voxel == r + 1 - dy, spread[dy], block)
                band[
                    dz,
                    (r + lead) * in_width : (r + lead + 1) * in_width,
                    dx * 8 * CH : (dx + 1) * 8 * CH,
                ] = block.astype(bf16)


def convolve(padded, band, hidden, columns, band_rows):
    n = padded.shape[0]
    across = iota((n * ROWS, 8 * CH), 0) % WE
    for block in range(2):
        lo, width = columns[block]
        view = jnp.concatenate(
            [
                jnp.concatenate(
                    [padded[w, dz * WE : dz * WE + ROWS, lo : lo + width] for dz in range(3)],
                    axis=1,
                )
                for w in range(n)
            ],
            axis=0,
        )
        first = band_rows[block]
        weights = jnp.concatenate([band[dz, first : first + width, :] for dz in range(3)], axis=0)
        res = jnp.dot(view, weights, preferred_element_type=f32)
        before = pltpu.roll(res[:, : 8 * CH], 1, 0)
        after = pltpu.roll(res[:, 16 * CH :], n * ROWS - 1, 0)
        hidden[:, block * 8 * CH : (block + 1) * 8 * CH] = (
            res[:, 8 * CH : 16 * CH]
            + jnp.where(across == 0, 0.0, before)
            + jnp.where(across == WE - 1, 0.0, after)
        )


def group_sum(row):
    by = row.shape[1] // 2
    while by >= CH:
        row = row + pltpu.roll(row, by, 1)
        by //= 2
    return row


def normalize(hidden, gain, shift):
    voxels = float(WE * WE * WE)
    mean_value = group_sum(jnp.sum(hidden, axis=0, keepdims=True)) / voxels
    centered = hidden - mean_value
    variance = group_sum(jnp.sum(centered * centered, axis=0, keepdims=True)) / voxels
    scaled = centered * (lax.rsqrt(variance + epsilon) * gain) + shift
    return jnp.where(scaled >= 0, scaled, leak_slope * scaled).astype(bf16)


def decode_kernel(
    features,
    taps_first,
    gain_first,
    shift_first,
    taps_second,
    gain_second,
    shift_second,
    head_weight,
    head_bias,
    corners,
    counts,
    out,
    padded,
    normed,
    band_first,
    band_second,
    hidden,
    ext,
    sems,
):
    n = padded.shape[0]
    cin = padded.shape[2] // WE
    loads = [
        pltpu.make_async_copy(features.at[w], padded.at[w, WE : WE + ROWS, :], sems.at[w])
        for w in range(n)
    ]
    for load in loads:
        load.start()
    for w in range(n):
        padded[w, :WE, :] = jnp.zeros((WE, padded.shape[2]), bf16)
        padded[w, WE + ROWS :, :] = jnp.zeros((WE, padded.shape[2]), bf16)
        normed[w, :WE, :] = jnp.zeros((WE, normed.shape[2]), bf16)
        normed[w, WE + ROWS :, :] = jnp.zeros((WE, normed.shape[2]), bf16)
    ext[...] = jnp.zeros_like(ext)
    build_band(taps_first, band_first, cin, 2, True)
    build_band(taps_second, band_second, CH, 4, False)
    gains = [spread_lanes(g[...], WE * CH) for g in (gain_first, gain_second)]
    shifts = [spread_lanes(s[...], WE * CH) for s in (shift_first, shift_second)]
    for load in loads:
        load.wait()
    convolve(padded, band_first, hidden, ((0, 10 * cin), (6 * cin, 10 * cin)), (2 * cin, 0))
    for w in range(n):
        normed[w, WE : WE + ROWS, :] = normalize(
            hidden[w * ROWS : (w + 1) * ROWS, :], gains[0], shifts[0]
        )
    convolve(normed, band_second, hidden, ((0, 12 * CH), (4 * CH, 12 * CH)), (4 * CH, 0))

    tile = lax.axis_index("tiles")
    live_count = counts[lax.axis_index("sub"), tile]
    width = WE * CH
    pick_rows = one_hot(iota((width, CH), 0) % CH == iota((width, CH), 1)).astype(bf16)
    pick_lanes = one_hot(iota((CLASSES, LANES), 0) == iota((CLASSES, LANES), 1) % CLASSES)
    head_rows = lax.dot_general(
        pick_rows, head_weight[...], (((1,), (1,)), ((), ())), preferred_element_type=f32
    ).astype(bf16)
    head_full = jnp.dot(head_rows, pick_lanes.astype(bf16), preferred_element_type=f32)
    bias = spread_lanes(head_bias[...], LANES)
    head_gap = iota((width, LANES), 1) // CLASSES - iota((width, LANES), 0) // CH
    place_rows = iota((WE * EXT, ROWS), 0)
    place_cols = iota((WE * EXT, ROWS), 1)
    same_across = place_rows // EXT == place_cols % WE
    depth_gap = place_rows % EXT - place_cols // WE
    row_id = iota((WE * EXT, 1), 0)
    lane_id = iota((1, LANES), 1)
    center = (WE - 1) / 2.0
    spread = 2.0 * (WE / 4.0) ** 2
    for w in range(n):
        second = normalize(hidden[w * ROWS : (w + 1) * ROWS, :], gains[1], shifts[1])
        cz = corners[w, 0] - tile * TZ
        cx = corners[w, 1]
        cy = corners[w, 2]
        lane_tile = jnp.minimum(cy // 8, (VY - 24) // 8)
        rot = cy - lane_tile * 8
        placed = one_hot(same_across & (depth_gap == cz)).astype(bf16)
        moved = jnp.dot(placed, second, preferred_element_type=f32).astype(bf16)
        head = jnp.where(head_gap == rot, head_full, 0.0).astype(bf16)
        logits = jnp.dot(moved, head, preferred_element_type=f32) + bias
        z = row_id % EXT - cz
        across = (row_id // EXT).astype(f32) - center
        depth = z.astype(f32) - center
        gauss_rows = jnp.exp(-(depth * depth) / spread) * jnp.exp(-(across * across) / spread)
        gauss_rows = jnp.where((z >= 0) & (z < WE) & (w < live_count), gauss_rows, 0.0)
        y = lane_id // CLASSES - rot
        along = y.astype(f32) - center
        gauss_lanes = jnp.exp(-(along * along) / spread)
        gauss_lanes = jnp.where((y >= 0) & (y < WE), gauss_lanes, 0.0)
        weighted = (logits * (gauss_rows * gauss_lanes)).astype(bf16).astype(f32)
        lanes = pl.ds(pl.multiple_of(lane_tile * 128, 128), LANES)
        ext[pl.ds(cx, WE), :, lanes] += weighted.reshape(WE, EXT, LANES)
    out[...] = ext[...].astype(bf16)


def decode(features, taps_first, gf, sf, taps_second, gs, ss, hw, hb, corners, counts):
    n = features.shape[0]
    in_width = features.shape[-1]
    cin = in_width // WE
    vmem = pl.BlockSpec(memory_space=pltpu.VMEM)
    smem = pl.BlockSpec(memory_space=pltpu.SMEM)
    return pl.pallas_call(
        decode_kernel,
        out_shape=jax.ShapeDtypeStruct((VX, EXT, VY * CLASSES), bf16),
        in_specs=[pl.BlockSpec(memory_space=pltpu.HBM)] + [vmem] * 8 + [smem] * 2,
        out_specs=vmem,
        scratch_shapes=[
            pltpu.VMEM((n, ROWS + 2 * WE, in_width), bf16),
            pltpu.VMEM((n, ROWS + 2 * WE, WE * CH), bf16),
            pltpu.VMEM((3, 12 * cin, 24 * CH), bf16),
            pltpu.VMEM((3, 16 * CH, 24 * CH), bf16),
            pltpu.VMEM((n * ROWS, WE * CH), f32),
            pltpu.VMEM((VX, EXT, VY * CLASSES), f32),
            pltpu.SemaphoreType.DMA((n,)),
        ],
        compiler_params=pltpu.CompilerParams(vmem_limit_bytes=60 * 1024 * 1024),
    )(
        features.reshape(n, ROWS, in_width),
        taps_first.swapaxes(-1, -2).reshape(27 * CH, cin),
        gf,
        sf,
        taps_second.reshape(27 * CH, CH),
        gs,
        ss,
        hw.T,
        hb,
        corners,
        counts.T,
    )


def exchange_kernel(
    ext,
    out,
    got_sub,
    part,
    got_fold,
    tail,
    got_tail,
    sub_send,
    sub_recv,
    fold_send,
    fold_recv,
    tile_send,
    tile_recv,
):
    fold, sub, tile = (lax.axis_index(a) for a in ("folds", "sub", "tiles"))
    folds, subs, tiles = (lax.axis_size(a) for a in ("folds", "sub", "tiles"))
    span = out.shape[0]
    chunks = 2 if span % 2 == 0 else 1
    step = span // chunks
    mesh_id = pl.DeviceIdType.MESH
    barrier = pltpu.get_barrier_semaphore()

    def greet(where):
        pl.semaphore_signal(barrier, inc=1, device_id=where, device_id_type=mesh_id)

    for e in range(1, subs):
        greet({"sub": lax.rem(sub + e, subs)})
    for d in range(1, folds):
        greet({"folds": lax.rem(fold + d, folds)})

    @pl.when(tile < tiles - 1)
    def _():
        greet({"tiles": tile + 1})

    @pl.when(tile > 0)
    def _():
        greet({"tiles": tile - 1})

    peers = subs - 1 + folds - 1
    at_end = (tile == 0) | (tile == tiles - 1)

    @pl.when(at_end)
    def _():
        pl.semaphore_wait(barrier, peers + 1)

    @pl.when(jnp.logical_not(at_end))
    def _():
        pl.semaphore_wait(barrier, peers + 2)

    def own(d, of_sub, half, k):
        first = (lax.rem(fold + d, folds) * subs + of_sub) * span + k * step
        return ext.at[pl.ds(first, step), pl.ds(half * TZ, TZ), :]

    def rows(k):
        return pl.ds(k * step, step)

    order = list(range(1, folds)) + [0]
    to_sub = {}
    for group in (order[:-1], order[-1:]):
        for half in (1, 0):
            for d in group:
                for k in range(chunks):
                    for e in range(1, subs):
                        peer = lax.rem(sub + e, subs)
                        copy = pltpu.make_async_remote_copy(
                            src_ref=own(d, peer, half, k),
                            dst_ref=got_sub.at[e - 1, d, half, rows(k)],
                            send_sem=sub_send.at[e - 1, d, half, k],
                            recv_sem=sub_recv.at[e - 1, d, half, k],
                            device_id={"sub": peer},
                            device_id_type=mesh_id,
                        )
                        copy.start()
                        to_sub[e, d, half, k] = copy

    def chip_sum(d, half, k):
        total = own(d, sub, half, k)[...].astype(f32)
        for e in range(1, subs):
            to_sub[e, d, half, k].wait_recv()
            total = total + got_sub[e - 1, d, half, rows(k)].astype(f32)
        return total

    to_fold = {}
    for half in (1, 0):
        for d in range(1, folds):
            for k in range(chunks):
                part[d - 1, half, rows(k)] = chip_sum(d, half, k).astype(bf16)
                copy = pltpu.make_async_remote_copy(
                    src_ref=part.at[d - 1, half, rows(k)],
                    dst_ref=got_fold.at[d - 1, half, rows(k)],
                    send_sem=fold_send.at[d - 1, half, k],
                    recv_sem=fold_recv.at[d - 1, half, k],
                    device_id={"folds": lax.rem(fold + d, folds)},
                    device_id_type=mesh_id,
                )
                copy.start()
                to_fold[d, half, k] = copy

    def full_sum(half, k):
        total = chip_sum(0, half, k)
        for d in range(1, folds):
            to_fold[d, half, k].wait_recv()
            total = total + got_fold[d - 1, half, rows(k)].astype(f32)
        return total

    to_tile = [
        pltpu.make_async_remote_copy(
            src_ref=tail.at[rows(k)],
            dst_ref=got_tail.at[rows(k)],
            send_sem=tile_send.at[k],
            recv_sem=tile_recv.at[k],
            device_id={"tiles": lax.rem(tile + 1, tiles)},
            device_id_type=mesh_id,
        )
        for k in range(chunks)
    ]
    for k in range(chunks):
        tail[rows(k)] = full_sum(1, k).astype(bf16)

        @pl.when(tile < tiles - 1)
        def _():
            to_tile[k].start()

    for k in range(chunks):
        out[rows(k)] = full_sum(0, k)

    @pl.when(tile > 0)
    def _():
        for k in range(chunks):
            to_tile[k].wait_recv()
            out[rows(k)] += got_tail[rows(k)].astype(f32)

    for copy in list(to_sub.values()) + list(to_fold.values()):
        copy.wait_send()

    @pl.when(tile < tiles - 1)
    def _():
        for copy in to_tile:
            copy.wait_send()


def exchange(ext):
    folds, subs = lax.axis_size("folds"), lax.axis_size("sub")
    span = VX // (folds * subs)
    lanes = VY * CLASSES
    chunks = 2 if span % 2 == 0 else 1
    vmem = pl.BlockSpec(memory_space=pltpu.VMEM)
    dma = pltpu.SemaphoreType.DMA
    return pl.pallas_call(
        exchange_kernel,
        out_shape=jax.ShapeDtypeStruct((span, TZ, lanes), f32),
        in_specs=[vmem],
        out_specs=vmem,
        scratch_shapes=[
            pltpu.VMEM((subs - 1, folds, 2, span, TZ, lanes), bf16),
            pltpu.VMEM((folds - 1, 2, span, TZ, lanes), bf16),
            pltpu.VMEM((folds - 1, 2, span, TZ, lanes), bf16),
            pltpu.VMEM((span, TZ, lanes), bf16),
            pltpu.VMEM((span, TZ, lanes), bf16),
            dma((subs - 1, folds, 2, chunks)),
            dma((subs - 1, folds, 2, chunks)),
            dma((folds - 1, 2, chunks)),
            dma((folds - 1, 2, chunks)),
            dma((chunks,)),
            dma((chunks,)),
        ],
        compiler_params=pltpu.CompilerParams(
            collective_id=0, has_side_effects=True, vmem_limit_bytes=12 * 1024 * 1024
        ),
    )(ext)


def on_device(
    features,
    conv_first,
    gain_first,
    shift_first,
    conv_second,
    gain_second,
    shift_second,
    head_weight,
    head_bias,
    corners,
    counts,
):
    extended = decode(
        features[0],
        conv_first[0],
        gain_first,
        shift_first,
        conv_second[0],
        gain_second,
        shift_second,
        head_weight[0],
        head_bias,
        corners,
        counts,
    )
    return exchange(extended).transpose(1, 0, 2)


def solution(mesh):
    placed = (
        P("folds", ("groups", "tiles", "sub"), None, None, None),
        P("folds", None, None, None, None, None),
        P("folds", None),
        P("folds", None),
        P("folds", None, None, None, None, None),
        P("folds", None),
        P("folds", None),
        P("folds", None, None),
        P("folds", None),
        P(("groups", "tiles", "sub"), None),
        P("groups", None),
    )
    return jax.shard_map(
        on_device,
        mesh=mesh,
        in_specs=placed,
        out_specs=P(("groups", "tiles"), ("folds", "sub"), None),
        check_vma=False,
    )
```
